128 devices in a mesh: band: 4 (over z_lo, core), facet: 32 (over z_hi, x, y).
Axes of the slice: x: 4, y: 4, z: 4 (z_hi: 2, z_lo: 2; z = z_hi * 2 + z_lo), core: 2. Of those that a mesh axis runs over, the one named last changes fastest.
Arguments:
- coeffs: float32 [4, 32, 256, 256], P('band', 'facet'), may hold values from -6 to 6
- dirty: float32 [16, 32, 256, 256], P('band', 'facet'), may hold values from -6 to 6
- psf: float32 [16, 32, 129, 129], P('band', 'facet'), may hold values from -0.046875 to 0.046875
- band_offset: float32 [16], P('band'), may hold values from -0.5 to 0.5
Outputs:
- gradient: float32 [4, 32, 256, 256], P('band', 'facet')
The draws below stay inside these ranges and needn't reach their ends.
All inputs are finite; a program needn't handle non-finite values.
Results may differ from the reference program's by a relative error of at most 0.0003.
Values sent between devices are 32-bit elements; how exact they have to be, the bound alone decides.
No kernel may reach another device: no remote copies, remote signals or barrier semaphores. Data moves between devices by JAX's collectives and lax.ppermute only.
A program may use at most 64 MiB of HBM per device.

```python
import jax
import jax.numpy as jnp
from jax import lax

P_SIZE = 256
B = 64
L = 512
BANDS = 16
TERMS = 4
FGY = 4
K = 129
FACETS = 32
FROWS = 8


def block_levels(stream_key, shape, pieces, smallest, high):
    gain, own = 1.0, jax.random.fold_in(stream_key, 6)
    for dim, parts in pieces:
        heights = jnp.exp(jax.random.uniform(jax.random.fold_in(own, dim), (parts,), jnp.float32, smallest / len(pieces), high / len(pieces)))
        gain = gain * jnp.repeat(heights, shape[dim] // parts).reshape([-1 if axis == dim else 1 for axis in range(len(shape))])
    return gain


def centred(rng, shape, spread, reach, shards=(), kind=jnp.bfloat16):
    array = jax.random.normal(rng, shape, jnp.float32) * spread
    if len(shards) > 0:
        array = block_levels(rng, shape, shards, -0.22, 0.18) * array
    return jnp.clip(array, min=-reach, max=reach).astype(kind)


def setup_inputs(seed: int = 0) -> dict:
    arg_keys = jax.random.split(jax.random.key(seed), 5)
    return {
        "coeffs": centred(arg_keys[0], (TERMS, FACETS, P_SIZE, P_SIZE), 1.0, 6.0, ((0, 4), (1, 32)), jnp.float32),
        "dirty": centred(arg_keys[1], (BANDS, FACETS, P_SIZE, P_SIZE), 1.0, 6.0, ((0, 4), (1, 32)), jnp.float32),
        "psf": centred(arg_keys[2], (BANDS, FACETS, K, K), (K * K) ** -0.5, 0.046875, ((0, 4), (1, 32)), jnp.float32),
        "band_offset": jnp.clip(jax.random.uniform(arg_keys[3], (BANDS,), jnp.float32, -0.5, 0.5) * block_levels(arg_keys[3], (BANDS,), ((0, 4),), -0.4, 0.0), -0.5, 0.5),
    }


def band_weights(band_offset):
    columns = [jnp.ones_like(band_offset)]
    for power in range(1, TERMS):
        columns.append(columns[-1] * band_offset)
    return jnp.stack(columns, axis=1)


def reference(coeffs, dirty, psf, band_offset):
    weights = band_weights(band_offset)
    span = P_SIZE + 2 * B
    offset = FGY + FGY // 2
    position = ((jnp.arange(FACETS) + offset) % FACETS).astype(jnp.int32)
    rows_idx = (position // FGY).astype(jnp.int32)
    cols_idx = (position % FGY).astype(jnp.int32)

    def one_band(carry, inputs):
        weight_row, dirty_band, psf_band = inputs
        model = jnp.einsum("t,tfij->fij", weight_row, coeffs, precision=lax.Precision.HIGHEST)
        placed = jnp.roll(model, offset, axis=0)
        sky = placed.reshape(FROWS, FGY, P_SIZE, P_SIZE).transpose(0, 2, 1, 3).reshape(FROWS * P_SIZE, FGY * P_SIZE)
        padded = jnp.pad(sky, B)

        def window(row, col):
            return lax.dynamic_slice(padded, ((row * P_SIZE).astype(jnp.int32), (col * P_SIZE).astype(jnp.int32)), (span, span))

        extended = jax.vmap(window)(rows_idx, cols_idx)
        ext_pad = jnp.pad(extended, ((0, 0), (0, L - span), (0, L - span)))
        kernel = jnp.pad(psf_band, ((0, 0), (0, L - K), (0, L - K)))
        kernel = jnp.roll(kernel, (-B, -B), axis=(1, 2))
        spectrum = jnp.fft.rfft2(ext_pad) * jnp.fft.rfft2(kernel)
        conv = jnp.fft.irfft2(spectrum, s=(L, L))
        smeared = conv[:, B:B + P_SIZE, B:B + P_SIZE].astype(carry.dtype)
        residual = dirty_band - smeared
        carry = carry + weight_row[:, None, None, None] * residual[None]
        return carry, None

    start = jnp.zeros((TERMS, FACETS, P_SIZE, P_SIZE), jnp.float32)
    gradient, unused = lax.scan(one_band, start, (weights, dirty, psf))
    return gradient
```

```python
import functools
import math

import jax
import jax.numpy as jnp
import ml_dtypes
import numpy as np
from jax import lax
from jax.experimental import pallas as pl
from jax.experimental.pallas import tpu as pltpu
from jax.sharding import PartitionSpec as P

P_SIZE = 256
B = 64
TERMS = 4
FGY = 4
FROWS = 8
FACETS = 32
K = 129
NR = 384
NC = 512
HR = NR // 2
HC = NC // 2
SPAN = P_SIZE + 2 * B
KP = 144

F32 = jnp.float32
BF16 = jnp.bfloat16


def basis(length, coords):
    freq = (np.arange(length // 2) + 0.5) * (2.0 * np.pi / length)
    angle = freq[:, None] * np.asarray(coords, np.float64)[None, :]
    return np.concatenate([np.cos(angle), np.sin(angle)], axis=0)


def halves(matrix):
    high = matrix.astype(np.float32).astype(ml_dtypes.bfloat16)
    low = (matrix - high.astype(np.float64)).astype(np.float32).astype(ml_dtypes.bfloat16)
    return high, low


@functools.cache
def tables():
    coords = np.concatenate([np.arange(P_SIZE + B), np.arange(-B, 0)])
    offsets = np.arange(KP) - B
    fc = basis(NC, coords).T
    fr = basis(NR, coords)
    gc = basis(NC, offsets[:K]).T
    gr = basis(NR, offsets) * (np.arange(KP) < K)[None, :]
    dc = basis(NC, np.arange(P_SIZE)) * (2.0 / NC)
    dr = basis(NR, np.arange(P_SIZE)).T * (2.0 / NR) * 0.5

    def right(m):
        h, l = halves(m)
        return np.concatenate([h, l], axis=0)

    def left(m):
        h, l = halves(m)
        return np.concatenate([h, l], axis=1)

    edge = np.zeros((8, NC), np.float32)
    edge[0] = gc[K - 1]
    return dict(
        fc=right(fc), fr=left(fr), gc=right(gc[:128]), gr=left(gr), dc=right(dc), dr=left(dr), edge=edge
    )


def split(x):
    high = x.astype(BF16)
    return high, (x - high.astype(F32)).astype(BF16)


def dot(a, b):
    return jnp.dot(a, b, preferred_element_type=F32)


def times(x, table):
    high, low = split(x)
    n = table.shape[0] // 2
    return dot(high, table[:n]) + (dot(low, table[:n]) + dot(high, table[n:]))


def under(table, x):
    high, low = split(x)
    n = table.shape[1] // 2
    return dot(table[:, :n], high) + (dot(table[:, :n], low) + dot(table[:, n:], high))


def diagonal(ref, cc, cs, sc, ss):
    ref[0, 0:HR, 0:HC] = cc - ss
    ref[0, HR:NR, 0:HC] = sc + cs
    ref[0, 0:HR, HC:NC] = cc + ss
    ref[0, HR:NR, HC:NC] = sc - cs


VMEM = pl.BlockSpec(memory_space=pltpu.VMEM)
SMEM = pl.BlockSpec(memory_space=pltpu.SMEM)
PARAMS = pltpu.CompilerParams(vmem_limit_bytes=48 * 1024 * 1024)


def shape(*dims, dtype=F32):
    return jax.ShapeDtypeStruct(dims, dtype)


def pack_kernel(odd_ref, x_ref, near_ref, far_ref):
    odd = odd_ref[0] == 1
    lane = lax.broadcasted_iota(jnp.int32, (128, 128), 1)
    left, right = x_ref[:, 0:128], x_ref[:, 128:256]
    left = jnp.where(lane < B, left[0:128], pltpu.roll(left[128:256], B, 1))
    right = jnp.where(lane < B, pltpu.roll(right[128:256], B, 1), right[0:128])
    near_ref[...] = jnp.where(odd, left, right)
    far_ref[...] = jnp.where(odd, right, left)


def pack(odd, x):
    return pl.pallas_call(
        pack_kernel,
        out_shape=(shape(128, 128), shape(128, 128)),
        in_specs=[SMEM, VMEM],
        out_specs=(VMEM, VMEM),
        compiler_params=PARAMS,
        name="pack",
    )(odd, x)


def widen_kernel(odd_ref, rowodd_ref, x_ref, near_ref, far_ref, wide_ref, near_out, far_out):
    odd = odd_ref[0] == 1
    rowodd = rowodd_ref[0] == 1
    lane = lax.broadcasted_iota(jnp.int32, (128, 128), 1)
    near, far = near_ref[...], far_ref[...]
    after = jnp.where(odd, far, near)
    before = jnp.where(odd, near, far)
    wide_ref[:, 0:256] = x_ref[...]
    wide_ref[0:128, 256:384] = jnp.where(lane < B, after, before)
    wide_ref[128:256, 256:384] = jnp.where(lane < B, pltpu.roll(after, B, 1), pltpu.roll(before, B, 1))
    top, bottom = wide_ref[0:B, :], wide_ref[256 - B : 256, :]
    near_out[...] = jnp.where(rowodd, top, bottom)
    far_out[...] = jnp.where(rowodd, bottom, top)


def widen(odd, rowodd, x, near, far):
    return pl.pallas_call(
        widen_kernel,
        out_shape=(shape(P_SIZE, SPAN), shape(B, SPAN), shape(B, SPAN)),
        in_specs=[SMEM, SMEM, VMEM, VMEM, VMEM],
        out_specs=(VMEM, VMEM, VMEM),
        compiler_params=PARAMS,
        name="widen",
    )(odd, rowodd, x, near, far)


def own_kernel(wide_ref, fc_ref, fr_ref, out_ref):
    cols = times(wide_ref[...], fc_ref[...])
    high, low = split(cols)
    fr_h, fr_l = fr_ref[:, 0:P_SIZE], fr_ref[:, NR : NR + P_SIZE]
    out_ref[...] = dot(fr_h, high) + (dot(fr_h, low) + dot(fr_l, high))


def own_rows(wide, fc, fr):
    return pl.pallas_call(
        own_kernel,
        out_shape=shape(NR, NC),
        in_specs=[VMEM] * 3,
        out_specs=VMEM,
        compiler_params=PARAMS,
        name="own_rows",
    )(wide, fc, fr)


def powers(offset, first):
    p = [None, offset]
    for _ in range(5):
        p.append(p[-1] * offset)
    p[0] = jnp.float32(1.0)
    return [
        jnp.where(first == 0, p[j], jnp.where(first == 1, p[j + 1], jnp.where(first == 2, p[j + 2], p[j + 3])))
        for j in range(TERMS)
    ]


def moments_kernel(term_ref, off_ref, offs_ref, psf_ref, psfs_ref, mine_ref, send_ref):
    offsets = [off_ref[b] for b in range(4)] + [offs_ref[b] for b in range(4)]
    kernels = [psf_ref.at[b] for b in range(4)] + [psfs_ref.at[b] for b in range(4)]
    for out_ref, first in ((mine_ref, term_ref[0]), (send_ref, term_ref[1])):
        w = [powers(o, first) for o in offsets]
        out_ref[:, 128:KP, :] = jnp.zeros((TERMS + 1, KP - 128, 128), F32)
        for start in range(0, K, 8):
            rows = min(8, K - start)
            main = [k[start : start + rows, 0:128] for k in kernels]
            edge = [k[start : start + rows, 128:129] for k in kernels]
            lane = lax.broadcasted_iota(jnp.int32, (rows, 128), 1)
            edges = jnp.zeros((rows, 128), F32)
            for j in range(TERMS):
                total, side = main[0] * w[0][j], edge[0] * w[0][j]
                for b in range(1, 8):
                    total = total + main[b] * w[b][j]
                    side = side + edge[b] * w[b][j]
                out_ref[j, start : start + rows, :] = total
                edges = jnp.where(lane == j, jnp.broadcast_to(side, (rows, 128)), edges)
            out_ref[TERMS, start : start + rows, :] = edges


def moments(terms, off, off_s, psf, psf_s):
    return pl.pallas_call(
        moments_kernel,
        out_shape=(shape(TERMS + 1, KP, 128), shape(TERMS + 1, KP, 128)),
        in_specs=[SMEM, SMEM, SMEM, VMEM, VMEM],
        out_specs=(VMEM, VMEM),
        compiler_params=PARAMS,
        name="moments",
    )(terms, off, off_s, psf, psf_s)


def kernels_kernel(mine_ref, got_ref, gc_ref, gr_ref, edge_ref, out_ref):
    side = mine_ref[TERMS] + got_ref[TERMS]
    last = edge_ref[0:1, :]
    q = (mine_ref[0] + got_ref[0])
    j = pl.program_id(0)
    q = mine_ref[j] + got_ref[j]
    lane = lax.broadcasted_iota(jnp.int32, (KP, 128), 1)
    column = jnp.sum(jnp.where(lane == j, side, 0.0), axis=1, keepdims=True)
    cols = times(q, gc_ref[...]) + column * last
    y = under(gr_ref[...], cols)
    diagonal(out_ref, y[0:HR, 0:HC], y[0:HR, HC:NC], y[HR:NR, 0:HC], y[HR:NR, HC:NC])


def kernel_spectra(mine, got, gc, gr, edge):
    return pl.pallas_call(
        kernels_kernel,
        grid=(TERMS,),
        out_shape=shape(TERMS, NR, NC),
        in_specs=[VMEM] * 5,
        out_specs=pl.BlockSpec((1, NR, NC), lambda j: (j, 0, 0)),
        compiler_params=PARAMS,
        name="kernel_spectra",
    )(mine, got, gc, gr, edge)


def dirty_kernel(off_ref, dirty_ref, out_ref):
    d = [dirty_ref[b] for b in range(4)]
    for t in range(TERMS):
        w = []
        for b in range(4):
            v = jnp.float32(1.0)
            for _ in range(t):
                v = v * off_ref[b]
            w.append(v)
        out_ref[t] = (d[0] * w[0] + d[1] * w[1]) + (d[2] * w[2] + d[3] * w[3])


def dirty_sums(off, dirty):
    rows = 64
    return pl.pallas_call(
        dirty_kernel,
        grid=(P_SIZE // rows,),
        out_shape=shape(TERMS, P_SIZE, P_SIZE),
        in_specs=[SMEM, pl.BlockSpec((4, rows, P_SIZE), lambda i: (0, i, 0))],
        out_specs=pl.BlockSpec((TERMS, rows, P_SIZE), lambda i: (0, i, 0)),
        compiler_params=PARAMS,
        name="dirty_sums",
    )(off, dirty)


def product_back(x_ref, y_ref, dirty_ref, dc_ref, dr_ref, z_ref, out_ref):
    a, b = x_ref[0, 0:HR, 0:HC], x_ref[0, HR:NR, 0:HC]
    c, d = y_ref[0, 0:HR, 0:HC], y_ref[0, HR:NR, 0:HC]
    rp, ip = a * c - b * d, a * d + b * c
    a, b = x_ref[0, 0:HR, HC:NC], x_ref[0, HR:NR, HC:NC]
    c, d = y_ref[0, 0:HR, HC:NC], y_ref[0, HR:NR, HC:NC]
    rm, im = a * c - b * d, a * d + b * c
    z_ref[0:HR, 0:HC] = rp + rm
    z_ref[0:HR, HC:NC] = ip - im
    z_ref[HR:NR, 0:HC] = ip + im
    z_ref[HR:NR, HC:NC] = rm - rp
    cols = times(z_ref[...], dc_ref[...])
    out_ref[...] = dirty_ref[0] - under(dr_ref[...], cols)


def first_kernel(idx_ref, own_ref, near_ref, far_ref, fc_ref, fr_ref, dc_ref, dr_ref, y0, y1, d0, d1,
                 x_ref, out0, out1, z_ref):
    rowodd = idx_ref[4] == 1
    near, far = near_ref[...], far_ref[...]
    halo = jnp.concatenate([jnp.where(rowodd, far, near), jnp.where(rowodd, near, far)], axis=0)
    cols = times(halo, fc_ref[...])
    high, low = split(cols)
    fr_h, fr_l = fr_ref[:, P_SIZE:NR], fr_ref[:, NR + P_SIZE :]
    x = own_ref[...] + (dot(fr_h, high) + (dot(fr_h, low) + dot(fr_l, high)))
    diagonal(x_ref, x[0:HR, 0:HC], x[0:HR, HC:NC], x[HR:NR, 0:HC], x[HR:NR, HC:NC])
    product_back(x_ref, y0, d0, dc_ref, dr_ref, z_ref, out0)
    product_back(x_ref, y1, d1, dc_ref, dr_ref, z_ref, out1)


def second_kernel(idx_ref, x_ref, dc_ref, dr_ref, y0, y1, d0, d1, out0, out1, z_ref):
    product_back(x_ref, y0, d0, dc_ref, dr_ref, z_ref, out0)
    product_back(x_ref, y1, d1, dc_ref, dr_ref, z_ref, out1)


def whole(*dims):
    return pl.BlockSpec(dims, lambda i, idx: (0,) * len(dims))


def pick(n, *dims):
    return pl.BlockSpec((1,) + dims, lambda i, idx: (idx[n],) + (0,) * len(dims))


def first(idx, own, near, far, fc, fr, dc, dr, y, dirty):
    return pl.pallas_call(
        first_kernel,
        grid_spec=pltpu.PrefetchScalarGridSpec(
            num_scalar_prefetch=1,
            grid=(1,),
            in_specs=[whole(*v.shape) for v in (own, near, far, fc, fr, dc, dr)]
            + [pick(0, NR, NC), pick(1, NR, NC), pick(0, P_SIZE, P_SIZE), pick(1, P_SIZE, P_SIZE)],
            out_specs=(whole(1, NR, NC), whole(P_SIZE, P_SIZE), whole(P_SIZE, P_SIZE)),
            scratch_shapes=[pltpu.VMEM((NR, NC), F32)],
        ),
        out_shape=(shape(1, NR, NC), shape(P_SIZE, P_SIZE), shape(P_SIZE, P_SIZE)),
        compiler_params=PARAMS,
        name="first",
    )(idx, own, near, far, fc, fr, dc, dr, y, y, dirty, dirty)


def second(idx, x, dc, dr, y, dirty):
    return pl.pallas_call(
        second_kernel,
        grid_spec=pltpu.PrefetchScalarGridSpec(
            num_scalar_prefetch=1,
            grid=(1,),
            in_specs=[whole(*v.shape) for v in (x, dc, dr)]
            + [pick(2, NR, NC), pick(3, NR, NC), pick(2, P_SIZE, P_SIZE), pick(3, P_SIZE, P_SIZE)],
            out_specs=(whole(P_SIZE, P_SIZE), whole(P_SIZE, P_SIZE)),
            scratch_shapes=[pltpu.VMEM((NR, NC), F32)],
        ),
        out_shape=(shape(P_SIZE, P_SIZE), shape(P_SIZE, P_SIZE)),
        compiler_params=PARAMS,
        name="second",
    )(idx, x, dc, dr, y, y, dirty, dirty)


OFFSET = FGY + FGY // 2


def facet_at(row, col):
    return (row * FGY + col - OFFSET) % FACETS


def exchanges():
    near_c, far_c, near_r, far_r = [], [], [], []
    for row in range(FROWS):
        for col in range(FGY):
            here = facet_at(row, col)
            if col + 1 < FGY:
                there = facet_at(row, col + 1)
                (near_c if here % 2 == 0 else far_c).extend([(here, there), (there, here)])
            if row + 1 < FROWS:
                there = facet_at(row + 1, col)
                (near_r if here // FGY % 2 == 0 else far_r).extend([(here, there), (there, here)])
    return near_c, far_c, near_r, far_r


CORES = [(0, 1), (1, 0), (2, 3), (3, 2)]
CHIPS = [(0, 2), (2, 0), (1, 3), (3, 1)]


def body(coeffs, dirty, psf, band_offset):
    table = {k: jnp.asarray(v) for k, v in tables().items()}
    near_c, far_c, near_r, far_r = exchanges()
    band, facet = lax.axis_index("band"), lax.axis_index("facet")
    chip, core = band // 2, band % 2
    other = (1 - chip) * 2
    odd = (facet % 2).reshape(1)
    rowodd = (facet // FGY % 2).reshape(1)
    idx = jnp.stack([other + core, other + 1 - core, band, chip * 2 + 1 - core, rowodd[0]])
    terms = jnp.stack([band, other + core])
    x = coeffs[0, 0]
    psf = psf[:, 0]

    psf_s = lax.ppermute(psf, "band", CORES)
    off_s = lax.ppermute(band_offset, "band", CORES)
    near, far = pack(odd, x)
    far = lax.ppermute(far, "facet", far_c)
    near = lax.ppermute(near, "facet", near_c)
    mine, send = moments(terms, band_offset, off_s, psf, psf_s)
    got = lax.ppermute(send, "band", CHIPS)
    wide, near, far = widen(odd, rowodd, x, near, far)
    far = lax.ppermute(far, "facet", far_r)
    near = lax.ppermute(near, "facet", near_r)
    own = own_rows(wide, table["fc"], table["fr"])
    y = kernel_spectra(mine, got, table["gc"], table["gr"], table["edge"])
    sums = dirty_sums(band_offset, dirty[:, 0])
    spec, same, cross = first(idx, own, near, far, table["fc"], table["fr"], table["dc"], table["dr"], y, sums)
    remote = same + lax.ppermute(cross, "band", CORES)
    remote = lax.ppermute(remote, "band", CHIPS)
    same, cross = second(idx, spec, table["dc"], table["dr"], y, sums)
    cross = lax.ppermute(cross, "band", CORES)
    return ((same + cross) + remote)[None, None]


def solution(mesh):
    placed = (
        P("band", "facet", None, None),
        P("band", "facet", None, None),
        P("band", "facet", None, None),
        P("band"),
    )
    return jax.shard_map(
        body, mesh=mesh, in_specs=placed, out_specs=P("band", "facet", None, None), check_vma=False
    )
```

```python
import functools

import jax
import jax.numpy as jnp
import ml_dtypes
import numpy as np
from jax import lax
from jax.experimental import pallas as pl
from jax.experimental.pallas import tpu as pltpu
from jax.sharding import PartitionSpec as P


P_SIZE = 256
B = 64
TERMS = 4
FGY = 4
FROWS = 8
FACETS = 32
K = 129
NR = 384
NC = 512
HR = NR // 2
HC = NC // 2
SPAN = P_SIZE + 2 * B
KP = 144
KW = 136
MOMENTS = 2 * TERMS - 1

F32 = jnp.float32
BF16 = jnp.bfloat16


def basis(length, coords):
    freq = (np.arange(length // 2) + 0.5) * (2.0 * np.pi / length)
    angle = freq[:, None] * np.asarray(coords, np.float64)[None, :]
    return np.concatenate([np.cos(angle), np.sin(angle)], axis=0)


def halves(matrix):
    high = matrix.astype(np.float32).astype(ml_dtypes.bfloat16)
    low = (matrix - high.astype(np.float64)).astype(np.float32).astype(ml_dtypes.bfloat16)
    return high, low


@functools.cache
def tables():
    coords = np.concatenate([np.arange(P_SIZE + B), np.arange(-B, 0)])
    offsets = np.arange(KP) - B
    fc = basis(NC, coords).T
    fr = basis(NR, coords)
    gc = basis(NC, offsets[:K]).T
    gr = basis(NR, offsets) * (np.arange(KP) < K)[None, :]
    dc = basis(NC, np.arange(P_SIZE)) * (2.0 / NC)
    dr = basis(NR, np.arange(P_SIZE)).T * (2.0 / NR) * 0.5

    def right(m):
        h, l = halves(m)
        return np.concatenate([h, l], axis=0)

    def left(m):
        h, l = halves(m)
        return np.concatenate([h, l], axis=1)

    edge = np.zeros((8, NC), np.float32)
    edge[0] = gc[K - 1]
    return dict(
        fc=right(fc), fr=left(fr), gc=right(gc[:128]), gr=left(gr), dc=right(dc), dr=left(dr), edge=edge
    )


def split(x):
    high = x.astype(BF16)
    return high, (x - high.astype(F32)).astype(BF16)


def dot(a, b):
    return jnp.dot(a, b, preferred_element_type=F32)


def times(x, table):
    high, low = split(x)
    n = table.shape[0] // 2
    return dot(
        jnp.concatenate([high, low, high], axis=1),
        jnp.concatenate([table[:n], table[:n], table[n:]], axis=0),
    )


def under(table, x):
    high, low = split(x)
    n = table.shape[1] // 2
    return mix(table[:, :n], table[:, n:], high, low)


def mix(left_high, left_low, high, low):
    return dot(
        jnp.concatenate([left_high, left_high, left_low], axis=1),
        jnp.concatenate([high, low, high], axis=0),
    )


def diagonal(ref, cc, cs, sc, ss):
    ref[0, 0:HR, 0:HC] = cc - ss
    ref[0, HR:NR, 0:HC] = sc + cs
    ref[0, 0:HR, HC:NC] = cc + ss
    ref[0, HR:NR, HC:NC] = sc - cs


VMEM = pl.BlockSpec(memory_space=pltpu.VMEM)
SMEM = pl.BlockSpec(memory_space=pltpu.SMEM)


def grant(mib):
    return pltpu.CompilerParams(vmem_limit_bytes=mib * 1024 * 1024)


def shape(*dims, dtype=F32):
    return jax.ShapeDtypeStruct(dims, dtype)


def pack_kernel(x_ref, near_ref, far_ref):
    odd = lax.axis_index("facet") % 2 == 1
    lane = lax.broadcasted_iota(jnp.int32, (128, 128), 1)
    left, right = x_ref[:, 0:128], x_ref[:, 128:256]
    left = jnp.where(lane < B, left[0:128], pltpu.roll(left[128:256], B, 1))
    right = jnp.where(lane < B, pltpu.roll(right[128:256], B, 1), right[0:128])
    near_ref[...] = jnp.where(odd, left, right)
    far_ref[...] = jnp.where(odd, right, left)


def pack(x):
    return pl.pallas_call(
        pack_kernel,
        out_shape=(shape(128, 128), shape(128, 128)),
        in_specs=[VMEM],
        out_specs=(VMEM, VMEM),
        compiler_params=grant(2),
        name="pack",
    )(x)


def side(near, far, half):
    lane = lax.broadcasted_iota(jnp.int32, near.shape, 1)
    odd = lax.axis_index("facet") % 2 == 1
    after, before = jnp.where(odd, far, near), jnp.where(odd, near, far)
    if half == 0:
        return jnp.where(lane < B, after, before)
    return jnp.where(lane < B, pltpu.roll(after, B, 1), pltpu.roll(before, B, 1))


def edges_kernel(x_ref, near_ref, far_ref, near_out, far_out):
    odd = lax.axis_index("facet") // FGY % 2 == 1
    top = side(near_ref[0:B, :], far_ref[0:B, :], 0)
    bottom = side(near_ref[B:, :], far_ref[B:, :], 1)
    for lanes, above, below in (
        (slice(0, 256), x_ref[0:B, :], x_ref[256 - B : 256, :]),
        (slice(256, 384), top, bottom),
    ):
        near_out[:, lanes] = jnp.where(odd, above, below)
        far_out[:, lanes] = jnp.where(odd, below, above)


def edges(x, near, far):
    return pl.pallas_call(
        edges_kernel,
        out_shape=(shape(B, SPAN), shape(B, SPAN)),
        in_specs=[VMEM] * 3,
        out_specs=(VMEM, VMEM),
        compiler_params=grant(2),
        name="edges",
    )(x, near, far)


def own_kernel(x_ref, near_ref, far_ref, fc_ref, fr_ref, out_ref):
    near, far = near_ref[...], far_ref[...]
    borders = jnp.concatenate([side(near, far, 0), side(near, far, 1)], axis=0)
    cols = times(jnp.concatenate([x_ref[...], borders], axis=1), fc_ref[...])
    high, low = split(cols)
    fr_h, fr_l = fr_ref[:, 0:P_SIZE], fr_ref[:, NR : NR + P_SIZE]
    out_ref[...] = mix(fr_h, fr_l, high, low)


def own_rows(*args):
    return pl.pallas_call(
        own_kernel,
        out_shape=shape(NR, NC),
        in_specs=[VMEM] * 5,
        out_specs=VMEM,
        compiler_params=grant(8),
        name="own_rows",
    )(*args)


def moments_kernel(off_ref, psf_ref, out_ref):
    weights = []
    for b in range(4):
        p = [jnp.float32(1.0)]
        for _ in range(MOMENTS - 1):
            p.append(p[-1] * off_ref[b])
        weights.append(p)
    lane = lax.broadcasted_iota(jnp.int32, (8, 128), 1)
    columns = []
    for start in range(0, 128, 8):
        main = [psf_ref[b, 0, start : start + 8, 0:128] for b in range(4)]
        edge = [psf_ref[b, 0, start : start + 8, 128:129] for b in range(4)]
        packed = jnp.zeros((8, 128), F32)
        for b in range(4):
            packed = jnp.where(lane == b, jnp.broadcast_to(edge[b], (8, 128)), packed)
        columns.append(packed)
        for s in range(MOMENTS):
            total = main[0] * weights[0][s]
            for b in range(1, 4):
                total = total + main[b] * weights[b][s]
            out_ref[s, start : start + 8, :] = total
    turned = jnp.concatenate(columns, axis=0).T
    last = [psf_ref[b, 0, 128:129, 0:128] for b in range(4)]
    corner = [jnp.broadcast_to(psf_ref[b, 0, 128:129, 128:129], (1, 128)) for b in range(4)]
    rest = jnp.zeros((5, 128), F32)
    for s in range(MOMENTS):
        rows = []
        for parts in (last, [turned[b : b + 1, :] for b in range(4)], corner):
            total = parts[0] * weights[0][s]
            for b in range(1, 4):
                total = total + parts[b] * weights[b][s]
            rows.append(total)
        out_ref[s, 128:KW, :] = jnp.concatenate(rows + [rest], axis=0)


def moments(off, psf):
    return pl.pallas_call(
        moments_kernel,
        out_shape=shape(MOMENTS, KW, 128),
        in_specs=[SMEM, VMEM],
        out_specs=VMEM,
        compiler_params=grant(4),
        name="moments",
    )(off, psf)


def terms():
    band = lax.axis_index("band")
    return band, (band + 2) % 4


def combine_kernel(mine_ref, got_ref, keep_ref, send_ref):
    own, other = terms()
    for j in range(TERMS):
        keep_ref[j] = mine_ref[own + j] + got_ref[own + j]
        send_ref[j] = mine_ref[other + j] + got_ref[other + j]


def combine(mine, got):
    return pl.pallas_call(
        combine_kernel,
        out_shape=(shape(TERMS, KW, 128), shape(TERMS, KW, 128)),
        in_specs=[VMEM, VMEM],
        out_specs=(VMEM, VMEM),
        compiler_params=grant(4),
        name="combine",
    )(mine, got)


def kernels_kernel(mine_ref, got_ref, gc_ref, gr_ref, edge_ref, out_ref):
    j = pl.program_id(0)
    q = mine_ref[j] + got_ref[j]
    pad = jnp.zeros((KP - KW, 128), F32)
    last = edge_ref[0:1, :]
    turned = jnp.concatenate([q[K : K + 1, :], jnp.zeros((127, 128), F32)], axis=0).T[:, 0:1]
    column = jnp.concatenate([turned, q[K + 1 : K + 2, 0:1], jnp.zeros((KP - K, 1), F32)], axis=0)
    cols = times(jnp.concatenate([q, pad], axis=0), gc_ref[...]) + column * last
    y = under(gr_ref[...], cols)
    diagonal(out_ref, y[0:HR, 0:HC], y[0:HR, HC:NC], y[HR:NR, 0:HC], y[HR:NR, HC:NC])


def kernel_spectra(*args):
    return pl.pallas_call(
        kernels_kernel,
        grid=(TERMS,),
        out_shape=shape(TERMS, NR, NC),
        in_specs=[VMEM] * 5,
        out_specs=pl.BlockSpec((1, NR, NC), lambda j: (j, 0, 0)),
        compiler_params=grant(12),
        name="kernel_spectra",
    )(*args)


def dirty_kernel(off_ref, dirty_ref, out_ref):
    d = [dirty_ref[b, 0] for b in range(4)]
    for t in range(TERMS):
        w = []
        for b in range(4):
            v = jnp.float32(1.0)
            for _ in range(t):
                v = v * off_ref[b]
            w.append(v)
        out_ref[t] = (d[0] * w[0] + d[1] * w[1]) + (d[2] * w[2] + d[3] * w[3])


def dirty_sums(off, dirty):
    rows = 64
    return pl.pallas_call(
        dirty_kernel,
        grid=(P_SIZE // rows,),
        out_shape=shape(TERMS, P_SIZE, P_SIZE),
        in_specs=[SMEM, pl.BlockSpec((4, 1, rows, P_SIZE), lambda i: (0, 0, i, 0))],
        out_specs=pl.BlockSpec((TERMS, rows, P_SIZE), lambda i: (0, i, 0)),
        compiler_params=grant(4),
        name="dirty_sums",
    )(off, dirty)


def target(chip, core):
    band = lax.axis_index("band")
    return (band // 2 + chip) % 2 * 2 + (band + core) % 2


def product_back(t, x_ref, y_ref, dirty_ref, dc_ref, dr_ref, z_ref):
    a, b = x_ref[0, 0:HR, 0:HC], x_ref[0, HR:NR, 0:HC]
    c, d = y_ref[t, 0:HR, 0:HC], y_ref[t, HR:NR, 0:HC]
    rp, ip = a * c - b * d, a * d + b * c
    a, b = x_ref[0, 0:HR, HC:NC], x_ref[0, HR:NR, HC:NC]
    c, d = y_ref[t, 0:HR, HC:NC], y_ref[t, HR:NR, HC:NC]
    rm, im = a * c - b * d, a * d + b * c
    z_ref[0:HR, 0:HC] = rp + rm
    z_ref[0:HR, HC:NC] = ip - im
    z_ref[HR:NR, 0:HC] = ip + im
    z_ref[HR:NR, HC:NC] = rm - rp
    cols = times(z_ref[...], dc_ref[...])
    return dirty_ref[t] - under(dr_ref[...], cols)


def first_kernel(own_ref, near_ref, far_ref, fc_ref, fr_ref, dc_ref, dr_ref, y_ref, dirty_ref,
                 x_ref, out_ref, z_ref):
    rowodd = lax.axis_index("facet") // FGY % 2 == 1
    near, far = near_ref[...], far_ref[...]
    halo = jnp.concatenate([jnp.where(rowodd, far, near), jnp.where(rowodd, near, far)], axis=0)
    cols = times(halo, fc_ref[...])
    high, low = split(cols)
    fr_h, fr_l = fr_ref[:, P_SIZE:NR], fr_ref[:, NR + P_SIZE :]
    x = own_ref[...] + mix(fr_h, fr_l, high, low)
    diagonal(x_ref, x[0:HR, 0:HC], x[0:HR, HC:NC], x[HR:NR, 0:HC], x[HR:NR, HC:NC])
    out_ref[...] = product_back(target(1, 1), x_ref, y_ref, dirty_ref, dc_ref, dr_ref, z_ref)


def first(*args):
    return pl.pallas_call(
        first_kernel,
        in_specs=[VMEM] * len(args),
        out_specs=(VMEM, VMEM),
        scratch_shapes=[pltpu.VMEM((NR, NC), F32)],
        out_shape=(shape(1, NR, NC), shape(P_SIZE, P_SIZE)),
        compiler_params=grant(12),
        name="first",
    )(*args)


def back_kernel(chip, core, x_ref, y_ref, dirty_ref, dc_ref, dr_ref, out_ref, z_ref):
    out_ref[...] = product_back(target(chip, core), x_ref, y_ref, dirty_ref, dc_ref, dr_ref, z_ref)


def back(chip, core, *args):
    return pl.pallas_call(
        functools.partial(back_kernel, chip, core),
        in_specs=[VMEM] * len(args),
        out_specs=VMEM,
        scratch_shapes=[pltpu.VMEM((NR, NC), F32)],
        out_shape=shape(P_SIZE, P_SIZE),
        compiler_params=grant(12),
    )(*args)


def total_kernel(*refs):
    value = refs[0][...]
    for ref in refs[1:-1]:
        value = value + ref[...]
    refs[-1][...] = value


def total(*args):
    return pl.pallas_call(
        total_kernel,
        out_shape=shape(P_SIZE, P_SIZE),
        in_specs=[VMEM] * len(args),
        out_specs=VMEM,
        compiler_params=grant(4),
    )(*args)


OFFSET = FGY + FGY // 2


def facet_at(row, col):
    return (row * FGY + col - OFFSET) % FACETS


def exchanges():
    near_c, far_c, near_r, far_r = [], [], [], []
    for row in range(FROWS):
        for col in range(FGY):
            here = facet_at(row, col)
            if col + 1 < FGY:
                there = facet_at(row, col + 1)
                (near_c if here % 2 == 0 else far_c).extend([(here, there), (there, here)])
            if row + 1 < FROWS:
                there = facet_at(row + 1, col)
                (near_r if here // FGY % 2 == 0 else far_r).extend([(here, there), (there, here)])
    return near_c, far_c, near_r, far_r


CORES = [(0, 1), (1, 0), (2, 3), (3, 2)]
CHIPS = [(0, 2), (2, 0), (1, 3), (3, 1)]


def body(coeffs, dirty, psf, band_offset):
    table = {k: jnp.asarray(v) for k, v in tables().items()}
    near_c, far_c, near_r, far_r = exchanges()
    x = coeffs[0, 0]
    near, far = pack(x)
    far = lax.ppermute(far, "facet", far_c)
    near = lax.ppermute(near, "facet", near_c)
    mine = moments(band_offset, psf)
    got = lax.ppermute(mine, "band", CORES)
    mine, send = combine(mine, got)
    got = lax.ppermute(send, "band", CHIPS)
    near_row, far_row = edges(x, near, far)
    far_row = lax.ppermute(far_row, "facet", far_r)
    near_row = lax.ppermute(near_row, "facet", near_r)
    own = own_rows(x, near, far, table["fc"], table["fr"])
    y = kernel_spectra(mine, got, table["gc"], table["gr"], table["edge"])
    sums = dirty_sums(band_offset, dirty)
    fixed = (y, sums, table["dc"], table["dr"])
    spec, cross = first(own, near_row, far_row, table["fc"], table["fr"], *fixed[2:], *fixed[:2])
    cross = lax.ppermute(cross, "band", CORES)
    remote = back(1, 0, spec, *fixed)
    remote = total(remote, cross)
    remote = lax.ppermute(remote, "band", CHIPS)
    cross = back(0, 1, spec, *fixed)
    cross = lax.ppermute(cross, "band", CORES)
    same = back(0, 0, spec, *fixed)
    return total(same, cross, remote)[None, None]


def solution(mesh):
    placed = (
        P("band", "facet", None, None),
        P("band", "facet", None, None),
        P("band", "facet", None, None),
        P("band"),
    )
    return jax.shard_map(
        body, mesh=mesh, in_specs=placed, out_specs=P("band", "facet", None, None), check_vma=False
    )
```

```python
import functools

import jax
import jax.numpy as jnp
import ml_dtypes
import numpy as np
from jax import lax
from jax.experimental import pallas as pl
from jax.experimental.pallas import tpu as pltpu
from jax.sharding import PartitionSpec as P


P_SIZE = 256
B = 64
TERMS = 4
FGY = 4
FROWS = 8
FACETS = 32
K = 129
NR = 384
NC = 512
HR = NR // 2
HC = NC // 2
SPAN = P_SIZE + 2 * B
KP = 144
KW = 136
MOMENTS = 2 * TERMS - 1
DIRTY_PARTS = 4

F32 = jnp.float32
BF16 = jnp.bfloat16


def basis(length, coords):
    freq = (np.arange(length // 2) + 0.5) * (2.0 * np.pi / length)
    angle = freq[:, None] * np.asarray(coords, np.float64)[None, :]
    return np.concatenate([np.cos(angle), np.sin(angle)], axis=0)


def halves(matrix):
    high = matrix.astype(np.float32).astype(ml_dtypes.bfloat16)
    low = (matrix - high.astype(np.float64)).astype(np.float32).astype(ml_dtypes.bfloat16)
    return high, low


@functools.cache
def tables():
    coords = np.concatenate([np.arange(P_SIZE + B), np.arange(-B, 0)])
    offsets = np.arange(KP) - B
    fc = basis(NC, coords).T
    fr = basis(NR, coords)
    gc = basis(NC, offsets[:K]).T
    gr = basis(NR, offsets) * (np.arange(KP) < K)[None, :]
    dc = basis(NC, np.arange(P_SIZE)) * (2.0 / NC)
    dr = basis(NR, np.arange(P_SIZE)).T * (2.0 / NR) * 0.5

    def right(m):
        h, l = halves(m)
        return np.concatenate([h, l], axis=0)

    def left(m):
        h, l = halves(m)
        return np.concatenate([h, l], axis=1)

    edge = np.zeros((8, NC), np.float32)
    edge[0] = gc[K - 1]
    return dict(
        fc=right(fc), fr=left(fr), gc=right(gc[:128]), gr=left(gr), dc=right(dc), dr=left(dr), edge=edge
    )


def split(x):
    high = x.astype(BF16)
    return high, (x - high.astype(F32)).astype(BF16)


def dot(a, b):
    return jnp.dot(a, b, preferred_element_type=F32)


def times(x, table):
    high, low = split(x)
    n = table.shape[0] // 2
    return dot(
        jnp.concatenate([high, low, high], axis=1),
        jnp.concatenate([table[:n], table[:n], table[n:]], axis=0),
    )


def under(table, x):
    high, low = split(x)
    n = table.shape[1] // 2
    return mix(table[:, :n], table[:, n:], high, low)


def mix(left_high, left_low, high, low):
    return dot(
        jnp.concatenate([left_high, left_high, left_low], axis=1),
        jnp.concatenate([high, low, high], axis=0),
    )


def diagonal(ref, cc, cs, sc, ss):
    ref[0, 0:HR, 0:HC] = cc - ss
    ref[0, HR:NR, 0:HC] = sc + cs
    ref[0, 0:HR, HC:NC] = cc + ss
    ref[0, HR:NR, HC:NC] = sc - cs


VMEM = pl.BlockSpec(memory_space=pltpu.VMEM)
SMEM = pl.BlockSpec(memory_space=pltpu.SMEM)
HBM = pl.BlockSpec(memory_space=pltpu.HBM)


def in_hbm(x):
    return pltpu.with_memory_space_constraint(x, pltpu.HBM)


def grant(mib):
    return pltpu.CompilerParams(vmem_limit_bytes=mib * 1024 * 1024)


def shape(*dims, dtype=F32):
    return jax.ShapeDtypeStruct(dims, dtype)


def pack_kernel(x_hbm, x_ref, near_ref, far_ref, sem):
    copy = pltpu.make_async_copy(x_hbm, x_ref, sem)
    copy.start()
    copy.wait()
    odd = lax.axis_index("facet") % 2 == 1
    lane = lax.broadcasted_iota(jnp.int32, (128, 128), 1)
    left, right = x_ref[:, 0:128], x_ref[:, 128:256]
    left = jnp.where(lane < B, left[0:128], pltpu.roll(left[128:256], B, 1))
    right = jnp.where(lane < B, pltpu.roll(right[128:256], B, 1), right[0:128])
    near_ref[...] = jnp.where(odd, left, right)
    far_ref[...] = jnp.where(odd, right, left)


def pack(x):
    return pl.pallas_call(
        pack_kernel,
        out_shape=(shape(P_SIZE, P_SIZE), shape(128, 128), shape(128, 128)),
        in_specs=[HBM],
        out_specs=(VMEM, VMEM, VMEM),
        scratch_shapes=[pltpu.SemaphoreType.DMA],
        compiler_params=grant(2),
        name="pack",
    )(x)


def side(near, far, half):
    lane = lax.broadcasted_iota(jnp.int32, near.shape, 1)
    odd = lax.axis_index("facet") % 2 == 1
    after, before = jnp.where(odd, far, near), jnp.where(odd, near, far)
    if half == 0:
        return jnp.where(lane < B, after, before)
    return jnp.where(lane < B, pltpu.roll(after, B, 1), pltpu.roll(before, B, 1))


def edges_kernel(x_ref, near_ref, far_ref, near_out, far_out):
    odd = lax.axis_index("facet") // FGY % 2 == 1
    top = side(near_ref[0:B, :], far_ref[0:B, :], 0)
    bottom = side(near_ref[B:, :], far_ref[B:, :], 1)
    for lanes, above, below in (
        (slice(0, 256), x_ref[0:B, :], x_ref[256 - B : 256, :]),
        (slice(256, 384), top, bottom),
    ):
        near_out[:, lanes] = jnp.where(odd, above, below)
        far_out[:, lanes] = jnp.where(odd, below, above)


def edges(x, near, far):
    return pl.pallas_call(
        edges_kernel,
        out_shape=(shape(B, SPAN), shape(B, SPAN)),
        in_specs=[VMEM] * 3,
        out_specs=(VMEM, VMEM),
        compiler_params=grant(2),
        name="edges",
    )(x, near, far)


def own_kernel(x_ref, near_ref, far_ref, fc_ref, fr_ref, out_ref):
    near, far = near_ref[...], far_ref[...]
    borders = jnp.concatenate([side(near, far, 0), side(near, far, 1)], axis=0)
    cols = times(jnp.concatenate([x_ref[...], borders], axis=1), fc_ref[...])
    high, low = split(cols)
    fr_h, fr_l = fr_ref[:, 0:P_SIZE], fr_ref[:, NR : NR + P_SIZE]
    out_ref[...] = mix(fr_h, fr_l, high, low)


def own_rows(*args):
    return pl.pallas_call(
        own_kernel,
        out_shape=shape(NR, NC),
        in_specs=[VMEM] * 5,
        out_specs=VMEM,
        compiler_params=grant(8),
        name="own_rows",
    )(*args)


def moments_kernel(off_hbm, psf_hbm, out_ref, off_ref, psf_ref, sems):
    copies = [pltpu.make_async_copy(psf_hbm.at[b, :, 0, :], psf_ref.at[b], sems.at[b]) for b in range(4)]
    copies.append(pltpu.make_async_copy(off_hbm, off_ref, sems.at[4]))
    for copy in copies:
        copy.start()
    for copy in copies:
        copy.wait()
    weights = []
    for b in range(4):
        p = [jnp.float32(1.0)]
        for _ in range(MOMENTS - 1):
            p.append(p[-1] * off_ref[b])
        weights.append(p)
    lane = lax.broadcasted_iota(jnp.int32, (8, 128), 1)
    columns = []
    for start in range(0, 128, 8):
        main = [psf_ref[b, start : start + 8, 0:128] for b in range(4)]
        edge = [psf_ref[b, start : start + 8, 128:129] for b in range(4)]
        packed = jnp.zeros((8, 128), F32)
        for b in range(4):
            packed = jnp.where(lane == b, jnp.broadcast_to(edge[b], (8, 128)), packed)
        columns.append(packed)
        for s in range(MOMENTS):
            total = main[0] * weights[0][s]
            for b in range(1, 4):
                total = total + main[b] * weights[b][s]
            out_ref[s, start : start + 8, :] = total
    turned = jnp.concatenate(columns, axis=0).T
    last = [psf_ref[b, 128:129, 0:128] for b in range(4)]
    corner = [jnp.broadcast_to(psf_ref[b, 128:129, 128:129], (1, 128)) for b in range(4)]
    rest = jnp.zeros((5, 128), F32)
    for s in range(MOMENTS):
        rows = []
        for parts in (last, [turned[b : b + 1, :] for b in range(4)], corner):
            total = parts[0] * weights[0][s]
            for b in range(1, 4):
                total = total + parts[b] * weights[b][s]
            rows.append(total)
        out_ref[s, 128:KW, :] = jnp.concatenate(rows + [rest], axis=0)


def moments(off, psf):
    return pl.pallas_call(
        moments_kernel,
        out_shape=shape(MOMENTS, KW, 128),
        in_specs=[HBM, HBM],
        out_specs=VMEM,
        scratch_shapes=[
            pltpu.SMEM((4,), F32),
            pltpu.VMEM((4, K, K), F32),
            pltpu.SemaphoreType.DMA((5,)),
        ],
        compiler_params=grant(4),
        name="moments",
    )(in_hbm(off), in_hbm(jnp.transpose(psf, (0, 2, 1, 3))))


def terms():
    band = lax.axis_index("band")
    return band, (band + 2) % 4


def combine_kernel(mine_ref, got_ref, keep_ref, send_ref):
    own, other = terms()
    for j in range(TERMS):
        keep_ref[j] = mine_ref[own + j] + got_ref[own + j]
        send_ref[j] = mine_ref[other + j] + got_ref[other + j]


def combine(mine, got):
    return pl.pallas_call(
        combine_kernel,
        out_shape=(shape(TERMS, KW, 128), shape(TERMS, KW, 128)),
        in_specs=[VMEM, VMEM],
        out_specs=(VMEM, VMEM),
        compiler_params=grant(4),
        name="combine",
    )(mine, got)


def kernels_kernel(mine_ref, got_ref, gc_ref, gr_ref, edge_ref, out_ref):
    j = pl.program_id(0)
    q = mine_ref[j] + got_ref[j]
    pad = jnp.zeros((KP - KW, 128), F32)
    last = edge_ref[0:1, :]
    turned = jnp.concatenate([q[K : K + 1, :], jnp.zeros((127, 128), F32)], axis=0).T[:, 0:1]
    column = jnp.concatenate([turned, q[K + 1 : K + 2, 0:1], jnp.zeros((KP - K, 1), F32)], axis=0)
    cols = times(jnp.concatenate([q, pad], axis=0), gc_ref[...]) + column * last
    y = under(gr_ref[...], cols)
    diagonal(out_ref, y[0:HR, 0:HC], y[0:HR, HC:NC], y[HR:NR, 0:HC], y[HR:NR, HC:NC])


def kernel_spectra(*args):
    return pl.pallas_call(
        kernels_kernel,
        grid=(TERMS,),
        out_shape=shape(TERMS, NR, NC),
        in_specs=[VMEM] * 5,
        out_specs=pl.BlockSpec((1, NR, NC), lambda j: (j, 0, 0)),
        compiler_params=grant(12),
        name="kernel_spectra",
    )(*args)


def dirty_kernel(off_hbm, dirty_hbm, out_ref, off_ref, dirty_ref, sems):
    copies = [pltpu.make_async_copy(off_hbm, off_ref, sems.at[DIRTY_PARTS])]
    rows = P_SIZE // DIRTY_PARTS
    for i in range(DIRTY_PARTS):
        part = pl.ds(i * rows, rows)
        copies.append(pltpu.make_async_copy(dirty_hbm.at[:, 0, part], dirty_ref.at[:, part], sems.at[i]))
    for copy in copies:
        copy.start()
    copies[0].wait()
    w = []
    for b in range(4):
        p = [jnp.float32(1.0)]
        for _ in range(TERMS - 1):
            p.append(p[-1] * off_ref[b])
        w.append(p)
    for i in range(DIRTY_PARTS):
        copies[i + 1].wait()
        for start in range(i * rows, (i + 1) * rows, 8):
            d = [dirty_ref[b, start : start + 8, :] for b in range(4)]
            for t in range(TERMS):
                out_ref[t, start : start + 8, :] = (d[0] * w[0][t] + d[1] * w[1][t]) + (
                    d[2] * w[2][t] + d[3] * w[3][t]
                )


def dirty_sums(off, dirty):
    return pl.pallas_call(
        dirty_kernel,
        out_shape=shape(TERMS, P_SIZE, P_SIZE),
        in_specs=[HBM, HBM],
        out_specs=VMEM,
        scratch_shapes=[
            pltpu.SMEM((4,), F32),
            pltpu.VMEM((4, P_SIZE, P_SIZE), F32),
            pltpu.SemaphoreType.DMA((DIRTY_PARTS + 1,)),
        ],
        compiler_params=grant(4),
        name="dirty_sums",
    )(in_hbm(off), in_hbm(dirty))


def target(chip, core):
    band = lax.axis_index("band")
    return (band // 2 + chip) % 2 * 2 + (band + core) % 2


def product_back(t, x_ref, y_ref, dirty_ref, dc_ref, dr_ref, z_ref):
    a, b = x_ref[0, 0:HR, 0:HC], x_ref[0, HR:NR, 0:HC]
    c, d = y_ref[t, 0:HR, 0:HC], y_ref[t, HR:NR, 0:HC]
    rp, ip = a * c - b * d, a * d + b * c
    a, b = x_ref[0, 0:HR, HC:NC], x_ref[0, HR:NR, HC:NC]
    c, d = y_ref[t, 0:HR, HC:NC], y_ref[t, HR:NR, HC:NC]
    rm, im = a * c - b * d, a * d + b * c
    z_ref[0:HR, 0:HC] = rp + rm
    z_ref[0:HR, HC:NC] = ip - im
    z_ref[HR:NR, 0:HC] = ip + im
    z_ref[HR:NR, HC:NC] = rm - rp
    cols = times(z_ref[...], dc_ref[...])
    return dirty_ref[t] - under(dr_ref[...], cols)


def first_kernel(own_ref, near_ref, far_ref, fc_ref, fr_ref, dc_ref, dr_ref, y_ref, dirty_ref,
                 x_ref, out_ref, z_ref):
    rowodd = lax.axis_index("facet") // FGY % 2 == 1
    near, far = near_ref[...], far_ref[...]
    halo = jnp.concatenate([jnp.where(rowodd, far, near), jnp.where(rowodd, near, far)], axis=0)
    cols = times(halo, fc_ref[...])
    high, low = split(cols)
    fr_h, fr_l = fr_ref[:, P_SIZE:NR], fr_ref[:, NR + P_SIZE :]
    x = own_ref[...] + mix(fr_h, fr_l, high, low)
    diagonal(x_ref, x[0:HR, 0:HC], x[0:HR, HC:NC], x[HR:NR, 0:HC], x[HR:NR, HC:NC])
    out_ref[...] = product_back(target(1, 1), x_ref, y_ref, dirty_ref, dc_ref, dr_ref, z_ref)


def first(*args):
    return pl.pallas_call(
        first_kernel,
        in_specs=[VMEM] * len(args),
        out_specs=(VMEM, VMEM),
        scratch_shapes=[pltpu.VMEM((NR, NC), F32)],
        out_shape=(shape(1, NR, NC), shape(P_SIZE, P_SIZE)),
        compiler_params=grant(12),
        name="first",
    )(*args)


def back_kernel(chip, core, x_ref, y_ref, dirty_ref, dc_ref, dr_ref, out_ref, z_ref):
    out_ref[...] = product_back(target(chip, core), x_ref, y_ref, dirty_ref, dc_ref, dr_ref, z_ref)


def back(chip, core, *args):
    return pl.pallas_call(
        functools.partial(back_kernel, chip, core),
        in_specs=[VMEM] * len(args),
        out_specs=VMEM,
        scratch_shapes=[pltpu.VMEM((NR, NC), F32)],
        out_shape=shape(P_SIZE, P_SIZE),
        compiler_params=grant(12),
    )(*args)


def total_kernel(*refs):
    value = refs[0][...]
    for ref in refs[1:-1]:
        value = value + ref[...]
    refs[-1][...] = value


def total(*args):
    return pl.pallas_call(
        total_kernel,
        out_shape=shape(P_SIZE, P_SIZE),
        in_specs=[VMEM] * len(args),
        out_specs=VMEM,
        compiler_params=grant(4),
    )(*args)


OFFSET = FGY + FGY // 2


def facet_at(row, col):
    return (row * FGY + col - OFFSET) % FACETS


def exchanges():
    near_c, far_c, near_r, far_r = [], [], [], []
    for row in range(FROWS):
        for col in range(FGY):
            here = facet_at(row, col)
            if col + 1 < FGY:
                there = facet_at(row, col + 1)
                (near_c if here % 2 == 0 else far_c).extend([(here, there), (there, here)])
            if row + 1 < FROWS:
                there = facet_at(row + 1, col)
                (near_r if here // FGY % 2 == 0 else far_r).extend([(here, there), (there, here)])
    return near_c, far_c, near_r, far_r


CORES = [(0, 1), (1, 0), (2, 3), (3, 2)]
CHIPS = [(0, 2), (2, 0), (1, 3), (3, 1)]


def body(coeffs, dirty, psf, band_offset):
    table = {k: jnp.asarray(v) for k, v in tables().items()}
    near_c, far_c, near_r, far_r = exchanges()
    x, near, far = pack(in_hbm(coeffs[0, 0]))
    far = lax.ppermute(far, "facet", far_c)
    near = lax.ppermute(near, "facet", near_c)
    mine = moments(band_offset, psf)
    got = lax.ppermute(mine, "band", CORES)
    mine, send = combine(mine, got)
    got = lax.ppermute(send, "band", CHIPS)
    near_row, far_row = edges(x, near, far)
    far_row = lax.ppermute(far_row, "facet", far_r)
    near_row = lax.ppermute(near_row, "facet", near_r)
    own = own_rows(x, near, far, table["fc"], table["fr"])
    y = kernel_spectra(mine, got, table["gc"], table["gr"], table["edge"])
    sums = dirty_sums(band_offset, dirty)
    fixed = (y, sums, table["dc"], table["dr"])
    spec, cross = first(own, near_row, far_row, table["fc"], table["fr"], *fixed[2:], *fixed[:2])
    cross = lax.ppermute(cross, "band", CORES)
    remote = back(1, 0, spec, *fixed)
    remote = total(remote, cross)
    remote = lax.ppermute(remote, "band", CHIPS)
    cross = back(0, 1, spec, *fixed)
    cross = lax.ppermute(cross, "band", CORES)
    same = back(0, 0, spec, *fixed)
    return total(same, cross, remote)[None, None]


def solution(mesh):
    placed = (
        P("band", "facet", None, None),
        P("band", "facet", None, None),
        P("band", "facet", None, None),
        P("band"),
    )
    return jax.shard_map(
        body, mesh=mesh, in_specs=placed, out_specs=P("band", "facet", None, None), check_vma=False
    )
```

```python
import functools

import jax
import jax.numpy as jnp
import ml_dtypes
import numpy as np
from jax import lax
from jax.experimental import pallas as pl
from jax.experimental.pallas import tpu as pltpu
from jax.sharding import PartitionSpec as P


P_SIZE = 256
B = 64
TERMS = 4
FGY = 4
FROWS = 8
FACETS = 32
K = 129
NR = 384
NC = 512
HR = NR // 2
HC = NC // 2
SPAN = P_SIZE + 2 * B
KP = 144
KW = 136
MOMENTS = 2 * TERMS - 1
OFFSET = FGY + FGY // 2
DIRTY_PARTS = 4

F32 = jnp.float32
BF16 = jnp.bfloat16


def basis(length, coords):
    freq = (np.arange(length // 2) + 0.5) * (2.0 * np.pi / length)
    angle = freq[:, None] * np.asarray(coords, np.float64)[None, :]
    return np.concatenate([np.cos(angle), np.sin(angle)], axis=0)


def halves(matrix):
    high = matrix.astype(np.float32).astype(ml_dtypes.bfloat16)
    low = (matrix - high.astype(np.float64)).astype(np.float32).astype(ml_dtypes.bfloat16)
    return high, low


@functools.cache
def tables():
    coords = np.concatenate([np.arange(P_SIZE + B), np.arange(-B, 0)])
    offsets = np.arange(KP) - B
    fc = basis(NC, coords).T
    fr = basis(NR, coords)
    gc = basis(NC, offsets[:K]).T
    gr = basis(NR, offsets) * (np.arange(KP) < K)[None, :]
    dc = basis(NC, np.arange(P_SIZE)) * (2.0 / NC)
    dr = basis(NR, np.arange(P_SIZE)).T * (2.0 / NR) * 0.5

    def right(m):
        h, l = halves(m)
        return np.concatenate([h, l], axis=0)

    def left(m):
        h, l = halves(m)
        return np.concatenate([h, l], axis=1)

    edge = np.zeros((8, NC), np.float32)
    edge[0] = gc[K - 1]
    return dict(
        fc=right(fc), fr=left(fr), gc=right(gc[:128]), gr=left(gr), dc=right(dc), dr=left(dr), edge=edge
    )


def split(x):
    high = x.astype(BF16)
    return high, (x - high.astype(F32)).astype(BF16)


def dot(a, b):
    return jnp.dot(a, b, preferred_element_type=F32)


def times(x, table):
    high, low = split(x)
    n = table.shape[0] // 2
    return dot(
        jnp.concatenate([high, low, high], axis=1),
        jnp.concatenate([table[:n], table[:n], table[n:]], axis=0),
    )


def under(table, x):
    high, low = split(x)
    n = table.shape[1] // 2
    return mix(table[:, :n], table[:, n:], high, low)


def mix(left_high, left_low, high, low):
    return dot(
        jnp.concatenate([left_high, left_high, left_low], axis=1),
        jnp.concatenate([high, low, high], axis=0),
    )


def diagonal(ref, cc, cs, sc, ss):
    ref[0, 0:HR, 0:HC] = cc - ss
    ref[0, HR:NR, 0:HC] = sc + cs
    ref[0, 0:HR, HC:NC] = cc + ss
    ref[0, HR:NR, HC:NC] = sc - cs


VMEM = pl.BlockSpec(memory_space=pltpu.VMEM)
SMEM = pl.BlockSpec(memory_space=pltpu.SMEM)
HBM = pl.BlockSpec(memory_space=pltpu.HBM)


def in_hbm(x):
    return pltpu.with_memory_space_constraint(x, pltpu.HBM)


def grant(mib):
    return pltpu.CompilerParams(vmem_limit_bytes=mib * 1024 * 1024)


def shape(*dims, dtype=F32):
    return jax.ShapeDtypeStruct(dims, dtype)


def pack_kernel(x_hbm, x_ref, near_ref, far_ref, sem):
    copies = []
    for start in range(0, P_SIZE, 32):
        part = pl.ds(start, 32)
        copies.append(pltpu.make_async_copy(x_hbm.at[part], x_ref.at[part], sem.at[start // 32]))
    for copy in copies:
        copy.start()
    for copy in copies:
        copy.wait()
    odd = lax.axis_index("facet") % 2 == 1
    lane = lax.broadcasted_iota(jnp.int32, (128, 128), 1)
    left, right = x_ref[:, 0:128], x_ref[:, 128:256]
    left = jnp.where(lane < B, left[0:128], pltpu.roll(left[128:256], B, 1))
    right = jnp.where(lane < B, pltpu.roll(right[128:256], B, 1), right[0:128])
    near_ref[...] = jnp.where(odd, left, right)
    far_ref[...] = jnp.where(odd, right, left)


def pack(x):
    return pl.pallas_call(
        pack_kernel,
        out_shape=(shape(P_SIZE, P_SIZE), shape(128, 128), shape(128, 128)),
        in_specs=[HBM],
        out_specs=(VMEM, VMEM, VMEM),
        scratch_shapes=[pltpu.SemaphoreType.DMA((P_SIZE // 32,))],
        compiler_params=grant(2),
        name="pack",
    )(x)


def side(near, far, half):
    lane = lax.broadcasted_iota(jnp.int32, near.shape, 1)
    facet = lax.axis_index("facet")
    odd = facet % 2 == 1
    column = (facet + OFFSET) % FGY
    far = jnp.where(jnp.logical_or(column == 0, column == FGY - 1), 0.0, far)
    after, before = jnp.where(odd, far, near), jnp.where(odd, near, far)
    if half == 0:
        return jnp.where(lane < B, after, before)
    return jnp.where(lane < B, pltpu.roll(after, B, 1), pltpu.roll(before, B, 1))


def edges_kernel(x_ref, near_ref, far_ref, near_out, far_out):
    odd = lax.axis_index("facet") // FGY % 2 == 1
    top = side(near_ref[0:B, :], far_ref[0:B, :], 0)
    bottom = side(near_ref[B:, :], far_ref[B:, :], 1)
    for lanes, above, below in (
        (slice(0, 256), x_ref[0:B, :], x_ref[256 - B : 256, :]),
        (slice(256, 384), top, bottom),
    ):
        near_out[:, lanes] = jnp.where(odd, above, below)
        far_out[:, lanes] = jnp.where(odd, below, above)


def edges(x, near, far):
    return pl.pallas_call(
        edges_kernel,
        out_shape=(shape(B, SPAN), shape(B, SPAN)),
        in_specs=[VMEM] * 3,
        out_specs=(VMEM, VMEM),
        compiler_params=grant(2),
        name="edges",
    )(x, near, far)


def own_kernel(x_ref, near_ref, far_ref, fc_ref, fr_ref, out_ref):
    near, far = near_ref[...], far_ref[...]
    borders = jnp.concatenate([side(near, far, 0), side(near, far, 1)], axis=0)
    cols = times(jnp.concatenate([x_ref[...], borders], axis=1), fc_ref[...])
    high, low = split(cols)
    fr_h, fr_l = fr_ref[:, 0:P_SIZE], fr_ref[:, NR : NR + P_SIZE]
    out_ref[...] = mix(fr_h, fr_l, high, low)


def own_rows(*args):
    return pl.pallas_call(
        own_kernel,
        out_shape=shape(NR, NC),
        in_specs=[VMEM] * 5,
        out_specs=VMEM,
        compiler_params=grant(8),
        name="own_rows",
    )(*args)


def moments_kernel(off_hbm, psf_hbm, out_ref, off_ref, psf_ref, sems):
    copies = [pltpu.make_async_copy(psf_hbm.at[b, :, 0, :], psf_ref.at[b], sems.at[b]) for b in range(4)]
    copies.append(pltpu.make_async_copy(off_hbm, off_ref, sems.at[4]))
    for copy in copies:
        copy.start()
    for copy in copies:
        copy.wait()
    weights = []
    for b in range(4):
        p = [jnp.float32(1.0)]
        for _ in range(MOMENTS - 1):
            p.append(p[-1] * off_ref[b])
        weights.append(p)
    lane = lax.broadcasted_iota(jnp.int32, (8, 128), 1)
    columns = []
    for start in range(0, 128, 8):
        main = [psf_ref[b, start : start + 8, 0:128] for b in range(4)]
        edge = [psf_ref[b, start : start + 8, 128:129] for b in range(4)]
        packed = jnp.zeros((8, 128), F32)
        for b in range(4):
            packed = jnp.where(lane == b, jnp.broadcast_to(edge[b], (8, 128)), packed)
        columns.append(packed)
        for s in range(MOMENTS):
            total = main[0] * weights[0][s]
            for b in range(1, 4):
                total = total + main[b] * weights[b][s]
            out_ref[s, start : start + 8, :] = total
    turned = jnp.concatenate(columns, axis=0).T
    last = [psf_ref[b, 128:129, 0:128] for b in range(4)]
    corner = [jnp.broadcast_to(psf_ref[b, 128:129, 128:129], (1, 128)) for b in range(4)]
    rest = jnp.zeros((5, 128), F32)
    for s in range(MOMENTS):
        rows = []
        for parts in (last, [turned[b : b + 1, :] for b in range(4)], corner):
            total = parts[0] * weights[0][s]
            for b in range(1, 4):
                total = total + parts[b] * weights[b][s]
            rows.append(total)
        out_ref[s, 128:KW, :] = jnp.concatenate(rows + [rest], axis=0)


def moments(off, psf):
    return pl.pallas_call(
        moments_kernel,
        out_shape=shape(MOMENTS, KW, 128),
        in_specs=[HBM, HBM],
        out_specs=VMEM,
        scratch_shapes=[
            pltpu.SMEM((4,), F32),
            pltpu.VMEM((4, K, K), F32),
            pltpu.SemaphoreType.DMA((5,)),
        ],
        compiler_params=grant(4),
        name="moments",
    )(in_hbm(off), in_hbm(jnp.transpose(psf, (0, 2, 1, 3))))


def terms():
    band = lax.axis_index("band")
    return band, (band + 2) % 4


def combine_kernel(mine_ref, got_ref, keep_ref, send_ref):
    own, other = terms()
    for j in range(TERMS):
        keep_ref[j] = mine_ref[own + j] + got_ref[own + j]
        send_ref[j] = mine_ref[other + j] + got_ref[other + j]


def combine(mine, got):
    return pl.pallas_call(
        combine_kernel,
        out_shape=(shape(TERMS, KW, 128), shape(TERMS, KW, 128)),
        in_specs=[VMEM, VMEM],
        out_specs=(VMEM, VMEM),
        compiler_params=grant(4),
        name="combine",
    )(mine, got)


def kernels_kernel(mine_ref, got_ref, gc_ref, gr_ref, edge_ref, out_ref):
    j = pl.program_id(0)
    q = mine_ref[j] + got_ref[j]
    pad = jnp.zeros((KP - KW, 128), F32)
    last = edge_ref[0:1, :]
    turned = jnp.concatenate([q[K : K + 1, :], jnp.zeros((127, 128), F32)], axis=0).T[:, 0:1]
    column = jnp.concatenate([turned, q[K + 1 : K + 2, 0:1], jnp.zeros((KP - K, 1), F32)], axis=0)
    cols = times(jnp.concatenate([q, pad], axis=0), gc_ref[...]) + column * last
    y = under(gr_ref[...], cols)
    diagonal(out_ref, y[0:HR, 0:HC], y[0:HR, HC:NC], y[HR:NR, 0:HC], y[HR:NR, HC:NC])


def kernel_spectra(*args):
    return pl.pallas_call(
        kernels_kernel,
        grid=(TERMS,),
        out_shape=shape(TERMS, NR, NC),
        in_specs=[VMEM] * 5,
        out_specs=pl.BlockSpec((1, NR, NC), lambda j: (j, 0, 0)),
        compiler_params=grant(12),
        name="kernel_spectra",
    )(*args)


def dirty_kernel(off_hbm, dirty_hbm, out_ref, off_ref, dirty_ref, sems):
    copies = [pltpu.make_async_copy(off_hbm, off_ref, sems.at[DIRTY_PARTS])]
    rows = P_SIZE // DIRTY_PARTS
    for i in range(DIRTY_PARTS):
        part = pl.ds(i * rows, rows)
        copies.append(pltpu.make_async_copy(dirty_hbm.at[:, 0, part], dirty_ref.at[:, part], sems.at[i]))
    for copy in copies:
        copy.start()
    copies[0].wait()
    w = []
    for b in range(4):
        p = [jnp.float32(1.0)]
        for _ in range(TERMS - 1):
            p.append(p[-1] * off_ref[b])
        w.append(p)
    for i in range(DIRTY_PARTS):
        copies[i + 1].wait()
        for start in range(i * rows, (i + 1) * rows, 8):
            d = [dirty_ref[b, start : start + 8, :] for b in range(4)]
            for t in range(TERMS):
                out_ref[t, start : start + 8, :] = (d[0] * w[0][t] + d[1] * w[1][t]) + (
                    d[2] * w[2][t] + d[3] * w[3][t]
                )


def dirty_sums(off, dirty):
    return pl.pallas_call(
        dirty_kernel,
        out_shape=shape(TERMS, P_SIZE, P_SIZE),
        in_specs=[HBM, HBM],
        out_specs=VMEM,
        scratch_shapes=[
            pltpu.SMEM((4,), F32),
            pltpu.VMEM((4, P_SIZE, P_SIZE), F32),
            pltpu.SemaphoreType.DMA((DIRTY_PARTS + 1,)),
        ],
        compiler_params=grant(4),
        name="dirty_sums",
    )(in_hbm(off), in_hbm(dirty))


def target(chip, core):
    band = lax.axis_index("band")
    return (band // 2 + chip) % 2 * 2 + (band + core) % 2


def product_back(t, x_ref, y_ref, dirty_ref, dc_ref, dr_ref, z_ref):
    a, b = x_ref[0, 0:HR, 0:HC], x_ref[0, HR:NR, 0:HC]
    c, d = y_ref[t, 0:HR, 0:HC], y_ref[t, HR:NR, 0:HC]
    rp, ip = a * c - b * d, a * d + b * c
    a, b = x_ref[0, 0:HR, HC:NC], x_ref[0, HR:NR, HC:NC]
    c, d = y_ref[t, 0:HR, HC:NC], y_ref[t, HR:NR, HC:NC]
    rm, im = a * c - b * d, a * d + b * c
    z_ref[0:HR, 0:HC] = rp + rm
    z_ref[0:HR, HC:NC] = ip - im
    z_ref[HR:NR, 0:HC] = ip + im
    z_ref[HR:NR, HC:NC] = rm - rp
    cols = times(z_ref[...], dc_ref[...])
    return dirty_ref[t] - under(dr_ref[...], cols)


def first_kernel(own_ref, near_ref, far_ref, fc_ref, fr_ref, dc_ref, dr_ref, y_ref, dirty_ref,
                 x_ref, out_ref, z_ref):
    facet = lax.axis_index("facet")
    odd = facet // FGY % 2 == 1
    row = (facet + OFFSET) % FACETS // FGY
    near, far = near_ref[...], far_ref[...]
    below = jnp.where(row == FROWS - 1, 0.0, jnp.where(odd, far, near))
    above = jnp.where(row == 0, 0.0, jnp.where(odd, near, far))
    halo = jnp.concatenate([below, above], axis=0)
    cols = times(halo, fc_ref[...])
    high, low = split(cols)
    fr_h, fr_l = fr_ref[:, P_SIZE:NR], fr_ref[:, NR + P_SIZE :]
    x = own_ref[...] + mix(fr_h, fr_l, high, low)
    diagonal(x_ref, x[0:HR, 0:HC], x[0:HR, HC:NC], x[HR:NR, 0:HC], x[HR:NR, HC:NC])
    out_ref[...] = product_back(target(1, 1), x_ref, y_ref, dirty_ref, dc_ref, dr_ref, z_ref)


def first(*args):
    return pl.pallas_call(
        first_kernel,
        in_specs=[VMEM] * len(args),
        out_specs=(VMEM, VMEM),
        scratch_shapes=[pltpu.VMEM((NR, NC), F32)],
        out_shape=(shape(1, NR, NC), shape(P_SIZE, P_SIZE)),
        compiler_params=grant(12),
        name="first",
    )(*args)


def back_kernel(chip, core, x_ref, y_ref, dirty_ref, dc_ref, dr_ref, out_ref, z_ref):
    out_ref[...] = product_back(target(chip, core), x_ref, y_ref, dirty_ref, dc_ref, dr_ref, z_ref)


def back(chip, core, *args):
    return pl.pallas_call(
        functools.partial(back_kernel, chip, core),
        in_specs=[VMEM] * len(args),
        out_specs=VMEM,
        scratch_shapes=[pltpu.VMEM((NR, NC), F32)],
        out_shape=shape(P_SIZE, P_SIZE),
        compiler_params=grant(12),
    )(*args)


def total_kernel(*refs):
    value = refs[0][...]
    for ref in refs[1:-1]:
        value = value + ref[...]
    refs[-1][...] = value


def total(*args):
    return pl.pallas_call(
        total_kernel,
        out_shape=shape(P_SIZE, P_SIZE),
        in_specs=[VMEM] * len(args),
        out_specs=VMEM,
        compiler_params=grant(4),
    )(*args)


def facet_at(row, col):
    return (row * FGY + col - OFFSET) % FACETS


def exchanges():
    near_c, far_c, near_r, far_r = [], [], [], []
    for row in range(FROWS):
        for col in range(FGY):
            here = facet_at(row, col)
            if col + 1 < FGY:
                there = facet_at(row, col + 1)
                (near_c if here % 2 == 0 else far_c).extend([(here, there), (there, here)])
            if row + 1 < FROWS:
                there = facet_at(row + 1, col)
                (near_r if here // FGY % 2 == 0 else far_r).extend([(here, there), (there, here)])
    for pairs in (near_c, far_c, near_r, far_r):
        alone = sorted(set(range(FACETS)) - {here for here, _ in pairs})
        for here, there in zip(alone[0::2], alone[1::2]):
            pairs.extend([(here, there), (there, here)])
    return near_c, far_c, near_r, far_r


CORES = [(0, 1), (1, 0), (2, 3), (3, 2)]
CHIPS = [(0, 2), (2, 0), (1, 3), (3, 1)]


def body(coeffs, dirty, psf, band_offset):
    table = {k: jnp.asarray(v) for k, v in tables().items()}
    near_c, far_c, near_r, far_r = exchanges()
    x, near, far = pack(in_hbm(coeffs[0, 0]))
    far = lax.ppermute(far, "facet", far_c)
    near = lax.ppermute(near, "facet", near_c)
    mine = moments(band_offset, psf)
    got = lax.ppermute(mine, "band", CORES)
    mine, send = combine(mine, got)
    got = lax.ppermute(send, "band", CHIPS)
    near_row, far_row = edges(x, near, far)
    far_row = lax.ppermute(far_row, "facet", far_r)
    near_row = lax.ppermute(near_row, "facet", near_r)
    own = own_rows(x, near, far, table["fc"], table["fr"])
    y = kernel_spectra(mine, got, table["gc"], table["gr"], table["edge"])
    sums = dirty_sums(band_offset, dirty)
    fixed = (y, sums, table["dc"], table["dr"])
    spec, cross = first(own, near_row, far_row, table["fc"], table["fr"], *fixed[2:], *fixed[:2])
    cross = lax.ppermute(cross, "band", CORES)
    remote = back(1, 0, spec, *fixed)
    remote = total(remote, cross)
    remote = lax.ppermute(remote, "band", CHIPS)
    cross = back(0, 1, spec, *fixed)
    cross = lax.ppermute(cross, "band", CORES)
    same = back(0, 0, spec, *fixed)
    return total(same, cross, remote)[None, None]


def solution(mesh):
    placed = (
        P("band", "facet", None, None),
        P("band", "facet", None, None),
        P("band", "facet", None, None),
        P("band"),
    )
    return jax.shard_map(
        body, mesh=mesh, in_specs=placed, out_specs=P("band", "facet", None, None), check_vma=False
    )
```

```python
import functools

import jax
import jax.numpy as jnp
import ml_dtypes
import numpy as np
from jax import lax
from jax.experimental import pallas as pl
from jax.experimental.pallas import tpu as pltpu
from jax.sharding import PartitionSpec as P


P_SIZE = 256
B = 64
TERMS = 4
FGY = 4
FROWS = 8
FACETS = 32
K = 129
NR = 384
NC = 512
HR = NR // 2
HC = NC // 2
SPAN = P_SIZE + 2 * B
KP = 144
KW = 136
MOMENTS = 2 * TERMS - 1
OFFSET = FGY + FGY // 2
DIRTY_PARTS = 4

F32 = jnp.float32
BF16 = jnp.bfloat16


def basis(length, coords):
    freq = (np.arange(length // 2) + 0.5) * (2.0 * np.pi / length)
    angle = freq[:, None] * np.asarray(coords, np.float64)[None, :]
    return np.concatenate([np.cos(angle), np.sin(angle)], axis=0)


def halves(matrix):
    high = matrix.astype(np.float32).astype(ml_dtypes.bfloat16)
    low = (matrix - high.astype(np.float64)).astype(np.float32).astype(ml_dtypes.bfloat16)
    return high, low


@functools.cache
def tables():
    coords = np.concatenate([np.arange(P_SIZE + B), np.arange(-B, 0)])
    offsets = np.arange(KP) - B
    fc = basis(NC, coords).T
    fr = basis(NR, coords)
    gc = basis(NC, offsets[:K]).T
    gr = basis(NR, offsets) * (np.arange(KP) < K)[None, :]
    dc = basis(NC, np.arange(P_SIZE)) * (2.0 / NC)
    dr = basis(NR, np.arange(P_SIZE)).T * (2.0 / NR) * 0.5

    def right(m):
        h, l = halves(m)
        return np.concatenate([h, l], axis=0)

    def left(m):
        h, l = halves(m)
        return np.concatenate([h, l], axis=1)

    edge = np.zeros((8, NC), np.float32)
    edge[0] = gc[K - 1]
    return dict(
        fc=right(fc), fr=left(fr), gc=right(gc[:128]), gr=left(gr), dc=right(dc), dr=left(dr), edge=edge
    )


def split(x):
    high = x.astype(BF16)
    return high, (x - high.astype(F32)).astype(BF16)


def dot(a, b):
    return jnp.dot(a, b, preferred_element_type=F32)


def times(x, table):
    high, low = split(x)
    n = table.shape[0] // 2
    return dot(
        jnp.concatenate([high, low, high], axis=1),
        jnp.concatenate([table[:n], table[:n], table[n:]], axis=0),
    )


def under(table, x):
    high, low = split(x)
    n = table.shape[1] // 2
    return mix(table[:, :n], table[:, n:], high, low)


def mix(left_high, left_low, high, low):
    return dot(
        jnp.concatenate([left_high, left_high, left_low], axis=1),
        jnp.concatenate([high, low, high], axis=0),
    )


def diagonal(ref, cc, cs, sc, ss):
    ref[0, 0:HR, 0:HC] = cc - ss
    ref[0, HR:NR, 0:HC] = sc + cs
    ref[0, 0:HR, HC:NC] = cc + ss
    ref[0, HR:NR, HC:NC] = sc - cs


VMEM = pl.BlockSpec(memory_space=pltpu.VMEM)
SMEM = pl.BlockSpec(memory_space=pltpu.SMEM)
HBM = pl.BlockSpec(memory_space=pltpu.HBM)


def in_hbm(x):
    return pltpu.with_memory_space_constraint(x, pltpu.HBM)


def grant(mib):
    return pltpu.CompilerParams(vmem_limit_bytes=mib * 1024 * 1024)


def shape(*dims, dtype=F32):
    return jax.ShapeDtypeStruct(dims, dtype)


def prepare_kernel(x_hbm, off_hbm, psf_hbm, x_ref, near_ref, far_ref, out_ref, off_ref, psf_ref, sems):
    image = pltpu.make_async_copy(x_hbm, x_ref, sems.at[0])
    copies = [pltpu.make_async_copy(off_hbm, off_ref, sems.at[1])]
    copies += [pltpu.make_async_copy(psf_hbm.at[b, :, 0, :], psf_ref.at[b], sems.at[2 + b]) for b in range(4)]
    image.start()
    for copy in copies:
        copy.start()
    image.wait()
    odd = lax.axis_index("facet") % 2 == 1
    lane = lax.broadcasted_iota(jnp.int32, (128, 128), 1)
    left, right = x_ref[:, 0:128], x_ref[:, 128:256]
    left = jnp.where(lane < B, left[0:128], pltpu.roll(left[128:256], B, 1))
    right = jnp.where(lane < B, pltpu.roll(right[128:256], B, 1), right[0:128])
    near_ref[...] = jnp.where(odd, left, right)
    far_ref[...] = jnp.where(odd, right, left)
    for copy in copies:
        copy.wait()
    weights = []
    for b in range(4):
        p = [jnp.float32(1.0)]
        for _ in range(MOMENTS - 1):
            p.append(p[-1] * off_ref[b])
        weights.append(p)
    lane = lax.broadcasted_iota(jnp.int32, (8, 128), 1)
    columns = []
    for start in range(0, 128, 8):
        main = [psf_ref[b, start : start + 8, 0:128] for b in range(4)]
        edge = [psf_ref[b, start : start + 8, 128:129] for b in range(4)]
        packed = jnp.zeros((8, 128), F32)
        for b in range(4):
            packed = jnp.where(lane == b, jnp.broadcast_to(edge[b], (8, 128)), packed)
        columns.append(packed)
        for s in range(MOMENTS):
            total = main[0] * weights[0][s]
            for b in range(1, 4):
                total = total + main[b] * weights[b][s]
            out_ref[s, start : start + 8, :] = total
    turned = jnp.concatenate(columns, axis=0).T
    last = [psf_ref[b, 128:129, 0:128] for b in range(4)]
    corner = [jnp.broadcast_to(psf_ref[b, 128:129, 128:129], (1, 128)) for b in range(4)]
    rest = jnp.zeros((5, 128), F32)
    for s in range(MOMENTS):
        rows = []
        for parts in (last, [turned[b : b + 1, :] for b in range(4)], corner):
            total = parts[0] * weights[0][s]
            for b in range(1, 4):
                total = total + parts[b] * weights[b][s]
            rows.append(total)
        out_ref[s, 128:KW, :] = jnp.concatenate(rows + [rest], axis=0)


def prepare(x, off, psf):
    return pl.pallas_call(
        prepare_kernel,
        out_shape=(shape(P_SIZE, P_SIZE), shape(128, 128), shape(128, 128), shape(MOMENTS, KW, 128)),
        in_specs=[HBM, HBM, HBM],
        out_specs=(VMEM,) * 4,
        scratch_shapes=[
            pltpu.SMEM((4,), F32),
            pltpu.VMEM((4, K, K), F32),
            pltpu.SemaphoreType.DMA((6,)),
        ],
        compiler_params=grant(4),
        name="prepare",
    )(in_hbm(x), in_hbm(off), in_hbm(jnp.transpose(psf, (0, 2, 1, 3))))


def side(near, far, half):
    lane = lax.broadcasted_iota(jnp.int32, near.shape, 1)
    facet = lax.axis_index("facet")
    odd = facet % 2 == 1
    column = (facet + OFFSET) % FGY
    far = jnp.where(jnp.logical_or(column == 0, column == FGY - 1), 0.0, far)
    after, before = jnp.where(odd, far, near), jnp.where(odd, near, far)
    if half == 0:
        return jnp.where(lane < B, after, before)
    return jnp.where(lane < B, pltpu.roll(after, B, 1), pltpu.roll(before, B, 1))


def edges_kernel(x_ref, near_ref, far_ref, near_out, far_out):
    odd = lax.axis_index("facet") // FGY % 2 == 1
    top = side(near_ref[0:B, :], far_ref[0:B, :], 0)
    bottom = side(near_ref[B:, :], far_ref[B:, :], 1)
    for lanes, above, below in (
        (slice(0, 256), x_ref[0:B, :], x_ref[256 - B : 256, :]),
        (slice(256, 384), top, bottom),
    ):
        near_out[:, lanes] = jnp.where(odd, above, below)
        far_out[:, lanes] = jnp.where(odd, below, above)


def edges(x, near, far):
    return pl.pallas_call(
        edges_kernel,
        out_shape=(shape(B, SPAN), shape(B, SPAN)),
        in_specs=[VMEM] * 3,
        out_specs=(VMEM, VMEM),
        compiler_params=grant(2),
        name="edges",
    )(x, near, far)


def own_kernel(x_ref, near_ref, far_ref, fc_ref, fr_ref, out_ref):
    near, far = near_ref[...], far_ref[...]
    borders = jnp.concatenate([side(near, far, 0), side(near, far, 1)], axis=0)
    cols = times(jnp.concatenate([x_ref[...], borders], axis=1), fc_ref[...])
    high, low = split(cols)
    fr_h, fr_l = fr_ref[:, 0:P_SIZE], fr_ref[:, NR : NR + P_SIZE]
    x = mix(fr_h, fr_l, high, low)
    diagonal(out_ref, x[0:HR, 0:HC], x[0:HR, HC:NC], x[HR:NR, 0:HC], x[HR:NR, HC:NC])


def own_rows(*args):
    return pl.pallas_call(
        own_kernel,
        out_shape=shape(1, NR, NC),
        in_specs=[VMEM] * 5,
        out_specs=VMEM,
        compiler_params=grant(8),
        name="own_rows",
    )(*args)


def target(chip, core):
    band = lax.axis_index("band")
    return (band // 2 + chip) % 2 * 2 + (band + core) % 2


def terms():
    band = lax.axis_index("band")
    return band, (band + 2) % 4


def combine_kernel(mine_ref, got_ref, leaves_ref, stays_ref, send_leaves_ref, send_stays_ref):
    own, other = terms()
    for core in range(2):
        for term, chip, ref in (
            (own, 1, leaves_ref),
            (own, 0, stays_ref),
            (other, 0, send_leaves_ref),
            (other, 1, send_stays_ref),
        ):
            s = term + target(chip, core)
            ref[core] = mine_ref[s] + got_ref[s]


def combine(mine, got):
    return pl.pallas_call(
        combine_kernel,
        out_shape=(shape(2, KW, 128),) * 4,
        in_specs=[VMEM, VMEM],
        out_specs=(VMEM,) * 4,
        compiler_params=grant(4),
        name="combine",
    )(mine, got)


def kernels_kernel(mine_ref, got_ref, gc_ref, gr_ref, edge_ref, out_ref):
    j = pl.program_id(0)
    q = mine_ref[j] + got_ref[j]
    pad = jnp.zeros((KP - KW, 128), F32)
    last = edge_ref[0:1, :]
    turned = jnp.concatenate([q[K : K + 1, :], jnp.zeros((127, 128), F32)], axis=0).T[:, 0:1]
    column = jnp.concatenate([turned, q[K + 1 : K + 2, 0:1], jnp.zeros((KP - K, 1), F32)], axis=0)
    cols = times(jnp.concatenate([q, pad], axis=0), gc_ref[...]) + column * last
    y = under(gr_ref[...], cols)
    diagonal(out_ref, y[0:HR, 0:HC], y[0:HR, HC:NC], y[HR:NR, 0:HC], y[HR:NR, HC:NC])


def kernel_spectra(*args):
    return pl.pallas_call(
        kernels_kernel,
        grid=(2,),
        out_shape=shape(2, NR, NC),
        in_specs=[VMEM] * 5,
        out_specs=pl.BlockSpec((1, NR, NC), lambda j: (j, 0, 0)),
        compiler_params=grant(12),
        name="kernel_spectra",
    )(*args)


def dirty_kernel(off_hbm, dirty_hbm, out_ref, off_ref, dirty_ref, sems):
    copies = [pltpu.make_async_copy(off_hbm, off_ref, sems.at[DIRTY_PARTS])]
    rows = P_SIZE // DIRTY_PARTS
    for i in range(DIRTY_PARTS):
        part = pl.ds(i * rows, rows)
        copies.append(pltpu.make_async_copy(dirty_hbm.at[:, 0, part], dirty_ref.at[:, part], sems.at[i]))
    for copy in copies:
        copy.start()
    copies[0].wait()
    w = []
    for b in range(4):
        p = [jnp.float32(1.0)]
        for _ in range(TERMS - 1):
            p.append(p[-1] * off_ref[b])
        w.append(p)
    for i in range(DIRTY_PARTS):
        copies[i + 1].wait()
        for start in range(i * rows, (i + 1) * rows, 8):
            d = [dirty_ref[b, start : start + 8, :] for b in range(4)]
            for t in range(TERMS):
                out_ref[t, start : start + 8, :] = (d[0] * w[0][t] + d[1] * w[1][t]) + (
                    d[2] * w[2][t] + d[3] * w[3][t]
                )


def dirty_sums(off, dirty):
    return pl.pallas_call(
        dirty_kernel,
        out_shape=shape(TERMS, P_SIZE, P_SIZE),
        in_specs=[HBM, HBM],
        out_specs=VMEM,
        scratch_shapes=[
            pltpu.SMEM((4,), F32),
            pltpu.VMEM((4, P_SIZE, P_SIZE), F32),
            pltpu.SemaphoreType.DMA((DIRTY_PARTS + 1,)),
        ],
        compiler_params=grant(4),
        name="dirty_sums",
    )(in_hbm(off), in_hbm(dirty))


ALL = ((0, P_SIZE),)
MIDDLE = ((B, P_SIZE - B),)
OUTER = ((0, B), (P_SIZE - B, P_SIZE))


def product_back(rows, chip, core, x_ref, y_ref, dirty_ref, dc_ref, dr_ref, out_ref, z_ref):
    a, b = x_ref[0, 0:HR, 0:HC], x_ref[0, HR:NR, 0:HC]
    c, d = y_ref[core, 0:HR, 0:HC], y_ref[core, HR:NR, 0:HC]
    rp, ip = a * c - b * d, a * d + b * c
    a, b = x_ref[0, 0:HR, HC:NC], x_ref[0, HR:NR, HC:NC]
    c, d = y_ref[core, 0:HR, HC:NC], y_ref[core, HR:NR, HC:NC]
    rm, im = a * c - b * d, a * d + b * c
    z_ref[0:HR, 0:HC] = rp + rm
    z_ref[0:HR, HC:NC] = ip - im
    z_ref[HR:NR, 0:HC] = ip + im
    z_ref[HR:NR, HC:NC] = rm - rp
    cols = times(z_ref[...], dc_ref[...])
    smeared = under(jnp.concatenate([dr_ref[start:stop] for start, stop in rows], axis=0), cols)
    term, at = target(chip, core), 0
    for start, stop in rows:
        size = stop - start
        out_ref[at : at + size, :] = dirty_ref[term, start:stop, :] - smeared[at : at + size, :]
        at += size


def first_kernel(own_ref, near_ref, far_ref, fc_ref, fr_ref, y_ref, dirty_ref, dc_ref, dr_ref, x_ref, out_ref, z_ref):
    facet = lax.axis_index("facet")
    odd = facet // FGY % 2 == 1
    row = (facet + OFFSET) % FACETS // FGY
    near, far = near_ref[...], far_ref[...]
    below = jnp.where(row == FROWS - 1, 0.0, jnp.where(odd, far, near))
    above = jnp.where(row == 0, 0.0, jnp.where(odd, near, far))
    halo = jnp.concatenate([below, above], axis=0)
    cols = times(halo, fc_ref[...])
    high, low = split(cols)
    fr_h, fr_l = fr_ref[:, P_SIZE:NR], fr_ref[:, NR + P_SIZE :]
    x = mix(fr_h, fr_l, high, low)
    diagonal(x_ref, x[0:HR, 0:HC], x[0:HR, HC:NC], x[HR:NR, 0:HC], x[HR:NR, HC:NC])
    x_ref[...] = x_ref[...] + own_ref[...]
    product_back(OUTER, 1, 1, x_ref, y_ref, dirty_ref, dc_ref, dr_ref, out_ref, z_ref)


def first(*args):
    return pl.pallas_call(
        first_kernel,
        in_specs=[VMEM] * len(args),
        out_specs=(VMEM, VMEM),
        scratch_shapes=[pltpu.VMEM((NR, NC), F32)],
        out_shape=(shape(1, NR, NC), shape(2 * B, P_SIZE)),
        compiler_params=grant(12),
        name="first",
    )(*args)


def back(rows, chip, core, *args):
    return pl.pallas_call(
        functools.partial(product_back, rows, chip, core),
        in_specs=[VMEM] * len(args),
        out_specs=VMEM,
        scratch_shapes=[pltpu.VMEM((NR, NC), F32)],
        out_shape=shape(sum(stop - start for start, stop in rows), P_SIZE),
        compiler_params=grant(12),
    )(*args)


def add_kernel(a_ref, b_ref, out_ref):
    out_ref[...] = a_ref[...] + b_ref[...]


def add(a, b):
    return pl.pallas_call(
        add_kernel,
        out_shape=shape(*a.shape),
        in_specs=[VMEM, VMEM],
        out_specs=VMEM,
        compiler_params=grant(2),
        name="add",
    )(a, b)


def last_kernel(a_ref, b_ref, middle_ref, outer_ref, out_ref):
    for ref, rows in ((middle_ref, MIDDLE), (outer_ref, OUTER)):
        at = 0
        for start, stop in rows:
            size = stop - start
            out_ref[start:stop] = (a_ref[start:stop] + b_ref[start:stop]) + ref[at : at + size]
            at += size


def last(*args):
    return pl.pallas_call(
        last_kernel,
        out_shape=shape(P_SIZE, P_SIZE),
        in_specs=[VMEM] * 4,
        out_specs=VMEM,
        compiler_params=grant(2),
        name="last",
    )(*args)


def facet_at(row, col):
    return (row * FGY + col - OFFSET) % FACETS


def exchanges():
    near_c, far_c, near_r, far_r = [], [], [], []
    for row in range(FROWS):
        for col in range(FGY):
            here = facet_at(row, col)
            if col + 1 < FGY:
                there = facet_at(row, col + 1)
                (near_c if here % 2 == 0 else far_c).extend([(here, there), (there, here)])
            if row + 1 < FROWS:
                there = facet_at(row + 1, col)
                (near_r if here // FGY % 2 == 0 else far_r).extend([(here, there), (there, here)])
    for pairs in (near_c, far_c, near_r, far_r):
        alone = sorted(set(range(FACETS)) - {here for here, _ in pairs})
        for here, there in zip(alone[0::2], alone[1::2]):
            pairs.extend([(here, there), (there, here)])
    return near_c, far_c, near_r, far_r


CORES = [(0, 1), (1, 0), (2, 3), (3, 2)]
CHIPS = [(0, 2), (2, 0), (1, 3), (3, 1)]


def body(coeffs, dirty, psf, band_offset):
    table = {k: jnp.asarray(v) for k, v in tables().items()}
    near_c, far_c, near_r, far_r = exchanges()
    x, near, far, mine = prepare(coeffs[0, 0], band_offset, psf)
    got = lax.ppermute(mine, "band", CORES)
    far = lax.ppermute(far, "facet", far_c)
    near = lax.ppermute(near, "facet", near_c)
    leaves, stays, send_leaves, send_stays = combine(mine, got)
    got_leaves = lax.ppermute(send_leaves, "band", CHIPS)
    got_stays = lax.ppermute(send_stays, "band", CHIPS)
    sums = dirty_sums(band_offset, dirty)
    near_row, far_row = edges(x, near, far)
    far_row = lax.ppermute(far_row, "facet", far_r)
    near_row = lax.ppermute(near_row, "facet", near_r)
    own = own_rows(x, near, far, table["fc"], table["fr"])
    fixed = (table["gc"], table["gr"], table["edge"])
    y = kernel_spectra(leaves, got_leaves, *fixed)
    rest = (sums, table["dc"], table["dr"])
    cross = back(MIDDLE, 1, 1, own, y, *rest)
    cross = lax.ppermute(cross, "band", CORES)
    middle = back(MIDDLE, 1, 0, own, y, *rest)
    middle = add(middle, cross)
    middle = lax.ppermute(middle, "band", CHIPS)
    spec, cross = first(own, near_row, far_row, table["fc"], table["fr"], y, *rest)
    cross = lax.ppermute(cross, "band", CORES)
    outer = back(OUTER, 1, 0, spec, y, *rest)
    outer = add(outer, cross)
    outer = lax.ppermute(outer, "band", CHIPS)
    y = kernel_spectra(stays, got_stays, *fixed)
    cross = back(ALL, 0, 1, spec, y, *rest)
    cross = lax.ppermute(cross, "band", CORES)
    same = back(ALL, 0, 0, spec, y, *rest)
    return last(same, cross, middle, outer)[None, None]


def solution(mesh):
    placed = (
        P("band", "facet", None, None),
        P("band", "facet", None, None),
        P("band", "facet", None, None),
        P("band"),
    )
    return jax.shard_map(
        body, mesh=mesh, in_specs=placed, out_specs=P("band", "facet", None, None), check_vma=False
    )
```
